128 devices in a mesh: delay: 4 (over z_hi, core), row: 4 (over x), col: 8 (over z_lo, y).
Axes of the slice: x: 4, y: 4, z: 4 (z_hi: 2, z_lo: 2; z = z_hi * 2 + z_lo), core: 2. Of those that a mesh axis runs over, the one named last changes fastest.
Arguments:
- operators: float32 [4, 9216, 9216], P('delay', 'col', 'row'), may hold values from -0.0625 to 0.0625
- excitation: float32 [3, 9216, 256], P(None, 'col'), may hold values from -6 to 6
- pending: float32 [4, 9216, 256], P('delay', 'col', 'row'), may hold values from -6 to 6
- sheet_gain: float32 [9216], P('row'), may hold values from 0.2 to 2
Outputs:
- currents: float32 [3, 9216, 256], P(None, 'row', 'col')
- remaining: float32 [4, 9216, 256], P('delay', 'col', 'row')
The draws below stay inside these ranges and needn't reach their ends.
All inputs are finite; a program needn't handle non-finite values.
Results may differ from the reference program's by a relative error of at most 0.00014.
Values sent between devices are 32-bit elements; how exact they have to be, the bound alone decides.
No kernel may reach another device: no remote copies, remote signals or barrier semaphores. Data moves between devices by JAX's collectives and lax.ppermute only.
A program may use at most 128 MiB of HBM per device.

```python
import math
import jax
import jax.numpy as jnp
from jax import lax

ORDER = 9216
COLUMNS = 256
STEPS = 3
DELAYS = 4


def steps_of(rng, shape, split, low, high):
    loudness = 1.0
    for position, shards_of in split:
        steps = jax.random.uniform(jax.random.fold_in(jax.random.fold_in(rng, 6), position), (shards_of,), jnp.float32, low / len(split), high / len(split))
        loudness = loudness * jnp.repeat(jnp.exp(steps), shape[position] // shards_of).reshape((-1,) + (1,) * (len(shape) - 1 - position))
    return loudness


def normal_values(key, shape, deviation, bound, split=(), kind=jnp.bfloat16):
    drawn = jax.random.normal(key, shape, jnp.float32) * deviation
    if len(split) > 0:
        drawn = steps_of(key, shape, split, -0.22, 0.18) * drawn
    return jnp.clip(drawn, min=-bound, max=bound).astype(kind)


def setup_inputs(seed: int = 0) -> dict:
    keys = jax.random.split(jax.random.key(seed), 5)
    return {
        "operators": normal_values(keys[0], (DELAYS, ORDER, ORDER), ORDER ** -0.5, 0.0625, ((0, 4), (1, 8), (2, 4)), jnp.float32),
        "excitation": normal_values(keys[1], (STEPS, ORDER, COLUMNS), 1.0, 6.0, ((1, 8),), jnp.float32),
        "pending": normal_values(keys[2], (DELAYS, ORDER, COLUMNS), 1.0, 6.0, ((0, 4), (1, 8), (2, 4)), jnp.float32),
        "sheet_gain": jnp.clip(jnp.exp(math.log(2.0) - 2.3025851 * jax.random.uniform(keys[3], (ORDER,), jnp.float32) ** steps_of(keys[3], (ORDER,), ((0, 4),), -0.2, 0.2)), 0.2, 2.0),
    }


def reference(operators, excitation, pending, sheet_gain):
    future = pending
    outputs = []
    for moment in range(STEPS):
        driving = excitation[moment] - future[0]
        sheet = jnp.dot(operators[0].T, driving, precision=lax.Precision.HIGHEST)
        current = sheet / (1.0 + sheet_gain[:, None] * sheet * sheet)
        outputs.append(current)
        updated = [future[0]]
        for delay_slot in range(1, DELAYS):
            updated.append(future[delay_slot] + jnp.dot(operators[delay_slot], current, precision=lax.Precision.HIGHEST))
        updated.append(jnp.zeros_like(future[0]))
        future = jnp.stack(updated[1:])
    return jnp.stack(outputs), future
```

```python
import jax
import jax.numpy as jnp
from jax import lax
from jax.sharding import PartitionSpec as P

STEPS = 3
SWAP = ((0, 1), (1, 0), (2, 3), (3, 2))
UP = ((0, 2), (1, 3))
DOWN = ((2, 0), (3, 1))


def product(x, w, over):
    return lax.dot_general(
        x,
        w,
        (((1,), (over,)), ((), ())),
        precision=lax.Precision.HIGH,
        preferred_element_type=jnp.float32,
    )


def sent_and_summed(x, axis):
    peers = lax.axis_size(axis)
    tiles = x.reshape(peers, x.shape[0] // peers, x.shape[1])
    return lax.all_to_all(tiles, axis, 0, 0, tiled=True).sum(axis=0)


def gathered(x, axis):
    peers = lax.axis_size(axis)
    tiles = jnp.broadcast_to(x[None], (peers, *x.shape))
    return lax.all_to_all(tiles, axis, 0, 0, tiled=True).reshape(peers * x.shape[0], x.shape[1])


def admitted(driving_part, operator, gain):
    driving = gathered(driving_part, "row")
    sheet = sent_and_summed(product(driving, operator, 0), "col")
    return sheet / (1.0 + gain * sheet * sheet)


def radiated(current_part, operator):
    return sent_and_summed(product(gathered(current_part, "col"), operator, 1), "row")


def radiated_twice(current_part, near, far):
    current = gathered(current_part, "col")
    columns, rows = current.shape[0], near.shape[0]
    peers = lax.axis_size("row")
    both = jnp.concatenate(
        [product(current, w, 1).reshape(peers, columns // peers, rows) for w in (near, far)], axis=1
    )
    summed = lax.all_to_all(both, "row", 0, 0, tiled=True).sum(axis=0)
    return summed[: columns // peers], summed[columns // peers :]


def local(operators, excitation, pending, sheet_gain):
    own = operators[0]
    testing, basis = own.shape
    delay = lax.axis_index("delay")
    core = delay % 2
    row = lax.axis_index("row")
    gain = sheet_gain[None, :]
    wide = pending.shape[2]
    half = 16
    groups = wide // (2 * half)

    def of_core(x, which):
        split = x.reshape(*x.shape[:-2], groups, 2, half, x.shape[-1])
        picked = lax.dynamic_index_in_dim(split, which, split.ndim - 3, keepdims=False)
        return picked.reshape(*x.shape[:-2], groups * half, x.shape[-1])

    def join(first, second):
        parts = [x.reshape(groups, 1, half, x.shape[-1]) for x in (first, second)]
        return jnp.concatenate(parts, axis=1).reshape(wide, first.shape[-1])

    due = pending[0].T
    mine = of_core(due, core)
    theirs = lax.ppermute(of_core(due, 1 - core), "delay", SWAP)
    even = jnp.where(core == 0, mine, theirs)
    odd = jnp.where(core == 0, theirs, mine)
    fresh = lax.dynamic_slice_in_dim(excitation, row * wide, wide, axis=2)
    fresh = of_core(jnp.swapaxes(fresh, 1, 2), core)
    own, even, odd = lax.optimization_barrier((own, even, odd))
    other = lax.ppermute(own, "delay", SWAP)

    keep = lambda value, *_: value
    blank = jnp.zeros((half, basis), jnp.float32)
    part = fresh[0] - even
    cur = lax.cond(delay == 0, lambda v, x, w: admitted(x, w, gain), keep, blank, part, own)
    currents, arrived = [], []
    near, far, late = [], [], []
    for moment in range(STEPS):
        if moment == 0:
            cur = lax.cond(delay == 1, lambda v, x, w: admitted(x, w, gain), keep, cur, part, other)
        else:
            cur = lax.switch(
                jnp.minimum(delay, 2),
                [
                    lambda v, x, a, b: admitted(x, a, gain),
                    lambda v, x, a, b: admitted(x, b, gain),
                    keep,
                ],
                blank, part, own, other,
            )
        currents.append(cur)
        sent = lax.ppermute(cur, "delay", UP)
        field = lax.switch(
            jnp.minimum(delay, 2),
            [
                lambda v, x, a, b: radiated(x, b),
                lambda v, x, a, b: radiated(x, a),
                keep,
            ],
            part, cur, own, other,
        )
        if moment == 0:
            part = fresh[1] - odd - field
        elif moment == 1:
            part = fresh[2] - late[0] - field
        else:
            part = field
        sent, part = lax.optimization_barrier((sent, part))
        arrived.append(sent)
        pair = lax.switch(
            jnp.maximum(delay - 1, 0),
            [
                lambda v, x, a, b: v,
                lambda v, x, a, b: radiated_twice(x, a, b),
                lambda v, x, a, b: radiated_twice(x, b, a),
            ],
            (part, part), sent, own, other,
        )
        near.append(pair[0])
        far.append(pair[1])
        if moment == 0:
            late.append(lax.ppermute(even + near[0], "delay", DOWN))
        elif moment == 1:
            late.append(lax.ppermute(odd + near[1] + far[0], "delay", DOWN))

    held = jnp.where(delay < 2, jnp.stack(currents), jnp.stack(arrived))
    swapped = lax.ppermute(held, "delay", SWAP)
    first = jnp.where(core == 0, held, swapped)
    second = jnp.where(core == 0, swapped, held)
    outputs = jnp.swapaxes(jnp.concatenate([first, second], axis=1), 1, 2)

    slot_zero = late[1] + part
    slot_one = near[2] + far[1]
    slot_two = far[2]
    leaving = jnp.where(delay == 1, slot_zero, jnp.where(delay == 2, slot_one, slot_two))
    came = lax.ppermute(leaving, "delay", ((1, 0), (2, 1), (3, 2)))
    crossed = lax.ppermute(slot_one, "delay", ((3, 1),))
    low = jnp.where(delay == 0, slot_zero, jnp.where(delay == 1, came, slot_two))
    high = jnp.where(delay == 1, crossed, came)
    remaining = jnp.where(delay < 3, join(low, high), 0.0)
    return outputs, remaining.T[None]


def solution(mesh):
    in_specs = (P("delay", "col", "row"), P(None, "col", None), P("delay", "col", "row"), P("row"))
    out_specs = (P(None, "row", "col"), P("delay", "col", "row"))
    return jax.shard_map(local, mesh=mesh, in_specs=in_specs, out_specs=out_specs, check_vma=False)
```

```python
import functools

import jax
import jax.numpy as jnp
from jax import lax
from jax.experimental import pallas as pl
from jax.experimental.pallas import tpu as pltpu
from jax.sharding import PartitionSpec as P

STEPS = 3
HALF = 16
SWAP = ((0, 1), (1, 0), (2, 3), (3, 2))
UP = ((0, 2), (1, 3))
DOWN = ((2, 0), (3, 1))


IN_VMEM = pl.BlockSpec(memory_space=pltpu.VMEM)
ANYWHERE = pl.BlockSpec(memory_space=pl.ANY)


def halves(x):
    high = x.astype(jnp.bfloat16)
    return high, (x - high.astype(jnp.float32)).astype(jnp.bfloat16)


def fetched(count, slots, sems, source):
    depth = slots.shape[0]

    def copy(i):
        slot = lax.rem(i, depth)
        return pltpu.make_async_copy(source(i), slots.at[slot], sems.at[slot])

    def start():
        for i in range(depth - 1):
            copy(i).start()

    def take(i):
        @pl.when(i + depth - 1 < count)
        def _():
            copy(i + depth - 1).start()

        copy(i).wait()
        return slots[lax.rem(i, depth)]

    return start, take


def both_halves(x_ref):
    groups, columns, length = x_ref.shape
    high, low = halves(x_ref[...].reshape(groups * columns, length))
    return high, jnp.concatenate([high, low], axis=0)


def multiplied(high, both, w, over):
    w_high, w_low = halves(w)
    over = (((1,), (over,)), ((), ()))
    main = lax.dot_general(both, w_high, over, preferred_element_type=jnp.float32)
    rest = lax.dot_general(high, w_low, over, preferred_element_type=jnp.float32)
    whole = high.shape[0]
    return main[:whole] + main[whole:] + rest


def admit_kernel(width, x_ref, w_ref, out_ref, *scratch):
    peers, part, basis = out_ref.shape
    count = basis // width

    def lanes(i):
        return pl.ds(pl.multiple_of(i * width, width), width)

    if scratch:
        start, take = fetched(count, *scratch, lambda i: w_ref.at[:, lanes(i)])
        start()
    else:
        take = lambda i: w_ref[:, lanes(i)]
    high, both = both_halves(x_ref)

    def body(i, _):
        out_ref[:, :, lanes(i)] = multiplied(high, both, take(i), 0).reshape(peers, part, width)
        return 0

    lax.fori_loop(0, count, body, 0)


def radiate_kernel(width, places, x_ref, *refs):
    kept_place, streamed_place = places
    refs = list(refs)
    kept_ref = refs.pop(0) if kept_place is not None else None
    streamed_ref = refs.pop(0) if streamed_place is not None else None
    out_ref, *scratch = refs
    peers, _, testing = out_ref.shape
    part = x_ref.shape[0] * x_ref.shape[1] // peers
    count, tail = divmod(testing, width)

    def rows(i, length):
        return pl.ds(pl.multiple_of(i * width, width), length)

    if scratch:
        slots, sems = scratch
        depth = slots.shape[0]

        def copy(i, length):
            slot = lax.rem(i, depth)
            source = streamed_ref.at[rows(i, length)]
            return pltpu.make_async_copy(source, slots.at[slot, pl.ds(0, length)], sems.at[slot])

        for i in range(depth - 1):
            copy(i, width).start()
    high, both = both_halves(x_ref)

    def put(place, i, length, w):
        total = multiplied(high, both, w, 1)
        if kept_place is not None and streamed_place is not None:
            core = lax.rem(lax.axis_index("delay"), 2)
            start = pl.multiple_of(part * (core if place == 0 else 1 - core), part)
        else:
            start = 0
        out_ref[:, pl.ds(start, part), rows(i, length)] = total.reshape(peers, part, length)

    if kept_place is not None:

        def kept_body(i, _):
            put(kept_place, i, width, kept_ref[rows(i, width), :])
            return 0

        lax.fori_loop(0, count, kept_body, 0)
        put(kept_place, count, tail, kept_ref[pl.ds(count * width, tail), :])
    if streamed_place is not None:

        def streamed_body(i, _):
            @pl.when(i + depth - 1 < count)
            def _():
                copy(i + depth - 1, width).start()

            @pl.when(i + depth - 1 == count)
            def _():
                copy(i + depth - 1, tail).start()

            copy(i, width).wait()
            put(streamed_place, i, width, slots[lax.rem(i, depth)])
            return 0

        lax.fori_loop(0, count, streamed_body, 0)
        copy(count, tail).wait()
        put(streamed_place, count, tail, slots[count % depth, pl.ds(0, tail), :])


LIMIT = pltpu.CompilerParams(vmem_limit_bytes=20 * 2**20)
LONG = pl.CostEstimate(flops=2 * 10**10, bytes_accessed=2**20, transcendentals=0)


def tiles(depth, shape):
    return [pltpu.VMEM((depth, *shape), jnp.float32), pltpu.SemaphoreType.DMA((depth,))]


def admit_product(x, operator, kept):
    testing, basis = operator.shape
    columns = x.shape[0] * x.shape[1]
    peers = lax.axis_size("col")
    width = 256
    return pl.pallas_call(
        functools.partial(admit_kernel, width),
        out_shape=jax.ShapeDtypeStruct((peers, columns // peers, basis), jnp.float32),
        in_specs=[IN_VMEM, IN_VMEM if kept else ANYWHERE],
        out_specs=IN_VMEM,
        scratch_shapes=[] if kept else tiles(4, (testing, width)),
        compiler_params=LIMIT,
        name="admit",
    )(x, operator)


def radiate_product(x, kept=None, streamed=None):
    given = [pair for pair in (kept, streamed) if pair is not None]
    testing, basis = given[0][0].shape
    columns = x.shape[0] * x.shape[1]
    peers = lax.axis_size("row")
    width = 256
    places = tuple(None if pair is None else pair[1] for pair in (kept, streamed))
    return pl.pallas_call(
        functools.partial(radiate_kernel, width, places),
        out_shape=jax.ShapeDtypeStruct((peers, len(given) * columns // peers, testing), jnp.float32),
        in_specs=[IN_VMEM] + [IN_VMEM] * (kept is not None) + [ANYWHERE] * (streamed is not None),
        out_specs=IN_VMEM,
        scratch_shapes=[] if streamed is None else tiles(3, (width, basis)),
        compiler_params=LIMIT,
        name="radiate",
    )(x, *[operator for operator, _ in given])


def spread_kernel(x_ref, out_ref):
    for i in range(out_ref.shape[0]):
        out_ref[i] = x_ref[...]


def spread(x, axis):
    return pl.pallas_call(
        spread_kernel,
        out_shape=jax.ShapeDtypeStruct((lax.axis_size(axis), *x.shape), x.dtype),
        in_specs=[IN_VMEM],
        out_specs=IN_VMEM,
        compiler_params=LIMIT,
        cost_estimate=LONG,
        name="spread",
    )(x)


def deduct_kernel(products_ref, given_ref, out_ref):
    row = lax.axis_index("row")
    for i in range(out_ref.shape[0]):
        out_ref[i] = jnp.where(row == i, given_ref[...], 0.0) - products_ref[i]


def deduct(products, given):
    return pl.pallas_call(
        deduct_kernel,
        out_shape=jax.ShapeDtypeStruct(products.shape, products.dtype),
        in_specs=[IN_VMEM, IN_VMEM],
        out_specs=IN_VMEM,
        compiler_params=LIMIT,
        cost_estimate=LONG,
        name="deduct",
    )(products, given)


def prepare_kernel(moments, wide, fresh_ref, *refs):
    *due_refs, slots, sems = refs
    row = lax.axis_index("row")
    core = lax.rem(lax.axis_index("delay"), 2)
    lanes = slots.shape[2]
    per = lanes // wide
    groups = wide // (2 * HALF)
    block = pl.ds(pl.multiple_of(row // per * lanes, lanes), lanes)
    copies = [
        pltpu.make_async_copy(fresh_ref.at[moment, :, block], slots.at[n], sems.at[n])
        for n, moment in enumerate(moments)
    ]
    for copy in copies:
        copy.start()

    def rows_of(ref, which, base):
        pieces = []
        for g in range(groups):
            start = pl.multiple_of(base + (2 * g + which) * HALF, HALF)
            pieces.append(ref[pl.ds(start, HALF), :])
        return jnp.concatenate(pieces, axis=0)

    if len(due_refs) > 2:
        due_ref, fresh_out, mine_out, leaving_out, turned = due_refs
        mine_out[...] = rows_of(due_ref, core, 0)
        leaving_out[...] = rows_of(due_ref, 1 - core, 0)
    else:
        fresh_out, turned = due_refs
    for n, copy in enumerate(copies):
        copy.wait()
        turned[...] = slots[n].T
        fresh_out[n] = rows_of(turned, core, lax.rem(row, per) * wide)


def prepared(excitation, moments, wide, due=None):
    testing = excitation.shape[1]
    half = jax.ShapeDtypeStruct((wide // 2, testing), jnp.float32)
    fresh = jax.ShapeDtypeStruct((len(moments), wide // 2, testing), jnp.float32)
    out = (fresh,) if due is None else (fresh, half, half)
    given = () if due is None else (due,)
    return pl.pallas_call(
        functools.partial(prepare_kernel, moments, wide),
        out_shape=out,
        in_specs=[ANYWHERE] + [IN_VMEM] * len(given),
        out_specs=(IN_VMEM,) * len(out),
        scratch_shapes=[
            pltpu.VMEM((128, testing), jnp.float32),
            pltpu.VMEM((len(moments), testing, 128), jnp.float32),
            pltpu.SemaphoreType.DMA((len(moments),)),
        ],
        compiler_params=LIMIT,
        name="prepare",
    )(excitation, *given)


def settle_kernel(parts_ref, gain_ref, out_ref):
    sheet = parts_ref[0]
    for i in range(1, parts_ref.shape[0]):
        sheet = sheet + parts_ref[i]
    out_ref[...] = sheet / (1.0 + gain_ref[...] * sheet * sheet)


def settled(parts, gain):
    return pl.pallas_call(
        settle_kernel,
        out_shape=jax.ShapeDtypeStruct(parts.shape[1:], parts.dtype),
        in_specs=[IN_VMEM, IN_VMEM],
        out_specs=IN_VMEM,
        compiler_params=LIMIT,
        name="settle",
    )(parts, gain)


def exchanged(x, axis):
    return lax.all_to_all(x, axis, 0, 0, tiled=True)


def gathered(x, axis):
    return exchanged(spread(x, axis), axis)


def admitted(driving, operator, gain, kept):
    return settled(exchanged(admit_product(driving, operator, kept), "col"), gain)


def radiated(current_part, **operators):
    return exchanged(radiate_product(gathered(current_part, "col"), **operators), "row").sum(axis=0)


def driven(products, given):
    size = lax.axis_size("row")
    total = deduct(products, given)
    near = [(i, i ^ 1) for i in range(size)]
    wrap = [(i, (i + 1 if i % 2 else i - 1) % size) for i in range(size)]
    first, second = total[: size // 2], total[size // 2 :]
    for one, two in ((near, wrap), (wrap, near)):
        came = lax.ppermute(first, "row", one), lax.ppermute(second, "row", two)
        first, second = first + came[0], second + came[1]
    return jnp.concatenate([first, second], axis=0)


def local(operators, excitation, pending, sheet_gain):
    own = operators[0]
    basis = own.shape[1]
    delay = lax.axis_index("delay")
    core = delay % 2
    gain = sheet_gain[None, :]
    wide = pending.shape[2]
    groups = wide // (2 * HALF)

    def join(first, second):
        parts = [x.reshape(groups, 1, HALF, x.shape[-1]) for x in (first, second)]
        return jnp.concatenate(parts, axis=1).reshape(wide, first.shape[-1])

    fresh, mine, leaving = prepared(excitation, (0,), wide, pending[0].T)
    theirs = lax.ppermute(leaving, "delay", SWAP)
    own, leaving = lax.optimization_barrier((own, leaving))
    other = lax.ppermute(own, "delay", SWAP)

    def keep(value, *_):
        return value

    def first_admitted(kept, v, x, y, w):
        return admitted(gathered(x - y, "row"), w, gain, kept)

    blank = jnp.zeros((HALF, basis), jnp.float32)
    cur = lax.cond(delay == 0, functools.partial(first_admitted, True), keep, blank, fresh[0], mine, own)
    excitation, cur = lax.optimization_barrier((excitation, cur))
    (later,) = prepared(excitation, (1, 2), wide)
    cur, other, theirs, later = lax.optimization_barrier((cur, other, theirs, later))
    even = jnp.where(core == 0, mine, theirs)
    odd = jnp.where(core == 0, theirs, mine)
    cur = lax.cond(delay == 1, functools.partial(first_admitted, False), keep, cur, fresh[0], theirs, other)
    which = jnp.minimum(delay, 2)
    currents, arrived = [], []
    near, far, late = [], [], []
    field = jnp.zeros((lax.axis_size("row"), wide // 2, pending.shape[1]), jnp.float32)
    for moment in range(STEPS):
        if moment > 0:
            given = later[moment - 1] - (odd if moment == 1 else late[0])
            cur = lax.switch(
                which,
                [
                    lambda v, x, g, a, b: admitted(driven(x, g), a, gain, True),
                    lambda v, x, g, a, b: admitted(driven(x, g), b, gain, False),
                    keep,
                ],
                blank, field, given, own, other,
            )
        currents.append(cur)
        sent = lax.ppermute(cur, "delay", UP)
        if moment == 1:
            late[0], cur = lax.optimization_barrier((late[0], cur))
        if moment == STEPS - 1:
            part = lax.switch(
                which,
                [
                    lambda v, x, a, b: radiated(x, streamed=(b, 0)),
                    lambda v, x, a, b: radiated(x, kept=(a, 0)),
                    keep,
                ],
                even, cur, own, other,
            )
            sent, done = lax.optimization_barrier((sent, part))
            start = jnp.concatenate([done, done], axis=0)
        else:
            field = lax.switch(
                which,
                [
                    lambda v, x, a, b: radiate_product(gathered(x, "col"), streamed=(b, 0)),
                    lambda v, x, a, b: radiate_product(gathered(x, "col"), kept=(a, 0)),
                    keep,
                ],
                field, cur, own, other,
            )
            sent, field = lax.optimization_barrier((sent, field))
            start = jnp.concatenate([even, odd], axis=0)
        arrived.append(sent)
        pair = lax.cond(
            delay >= 2,
            lambda v, x, a, b: radiated(x, kept=(a, 0), streamed=(b, 1)),
            keep,
            start, sent, own, other,
        )
        near.append(pair[: wide // 2])
        far.append(pair[wide // 2 :])
        if moment == 0:
            late.append(lax.ppermute(even + near[0], "delay", DOWN))
        elif moment == 1:
            late.append(lax.ppermute(odd + near[1] + far[0], "delay", DOWN))

    held = jnp.where(delay < 2, jnp.stack(currents), jnp.stack(arrived))
    swapped = lax.ppermute(held, "delay", SWAP)
    first = jnp.where(core == 0, held, swapped)
    second = jnp.where(core == 0, swapped, held)
    outputs = jnp.swapaxes(jnp.concatenate([first, second], axis=1), 1, 2)

    slot_zero = late[1] + part
    slot_one = near[2] + far[1]
    slot_two = far[2]
    leaving = jnp.where(delay == 1, slot_zero, jnp.where(delay == 2, slot_one, slot_two))
    came = lax.ppermute(leaving, "delay", ((1, 0), (2, 1), (3, 2)))
    crossed = lax.ppermute(slot_one, "delay", ((3, 1),))
    low = jnp.where(delay == 0, slot_zero, jnp.where(delay == 1, came, slot_two))
    high = jnp.where(delay == 1, crossed, came)
    remaining = jnp.where(delay < 3, join(low, high), 0.0)
    return outputs, remaining.T[None]


def solution(mesh):
    in_specs = (P("delay", "col", "row"), P(None, "col", None), P("delay", "col", "row"), P("row"))
    out_specs = (P(None, "row", "col"), P("delay", "col", "row"))
    return jax.shard_map(local, mesh=mesh, in_specs=in_specs, out_specs=out_specs, check_vma=False)
```

```python
import functools

import jax
import jax.numpy as jnp
from jax import lax
from jax.experimental import pallas as pl
from jax.experimental.pallas import tpu as pltpu
from jax.sharding import PartitionSpec as P

STEPS = 3
HALF = 16
SWAP = ((0, 1), (1, 0), (2, 3), (3, 2))
UP = ((0, 2), (1, 3))
DOWN = ((2, 0), (3, 1))


IN_VMEM = pl.BlockSpec(memory_space=pltpu.VMEM)
ANYWHERE = pl.BlockSpec(memory_space=pl.ANY)


def halves(x):
    high = x.astype(jnp.bfloat16)
    return high, (x - high.astype(jnp.float32)).astype(jnp.bfloat16)


def fetched(count, slots, sems, source):
    depth = slots.shape[0]

    def copy(i):
        slot = lax.rem(i, depth)
        return pltpu.make_async_copy(source(i), slots.at[slot], sems.at[slot])

    def start():
        for i in range(depth - 1):
            copy(i).start()

    def take(i):
        @pl.when(i + depth - 1 < count)
        def _():
            copy(i + depth - 1).start()

        copy(i).wait()
        return slots[lax.rem(i, depth)]

    return start, take


def both_halves(x_ref):
    groups, columns, length = x_ref.shape
    high, low = halves(x_ref[...].reshape(groups * columns, length))
    return high, jnp.concatenate([high, low], axis=0)


def multiplied(high, both, w, over):
    w_high, w_low = halves(w)
    over = (((1,), (over,)), ((), ()))
    main = lax.dot_general(both, w_high, over, preferred_element_type=jnp.float32)
    rest = lax.dot_general(high, w_low, over, preferred_element_type=jnp.float32)
    whole = high.shape[0]
    return main[:whole] + main[whole:] + rest


def admit_kernel(width, x_ref, w_ref, out_ref, *scratch):
    peers, part, basis = out_ref.shape
    count = basis // width

    def lanes(i):
        return pl.ds(pl.multiple_of(i * width, width), width)

    if scratch:
        start, take = fetched(count, *scratch, lambda i: w_ref.at[:, lanes(i)])
        start()
    else:
        take = lambda i: w_ref[:, lanes(i)]
    high, both = both_halves(x_ref)

    def body(i, _):
        out_ref[:, :, lanes(i)] = multiplied(high, both, take(i), 0).reshape(peers, part, width)
        return 0

    lax.fori_loop(0, count, body, 0)


def radiate_kernel(width, places, x_ref, *refs):
    kept_place, streamed_place = places
    refs = list(refs)
    kept_ref = refs.pop(0) if kept_place is not None else None
    streamed_ref = refs.pop(0) if streamed_place is not None else None
    out_ref, *scratch = refs
    peers, _, testing = out_ref.shape
    part = x_ref.shape[0] * x_ref.shape[1] // peers
    count, tail = divmod(testing, width)

    def rows(i, length):
        return pl.ds(pl.multiple_of(i * width, width), length)

    if scratch:
        slots, sems = scratch
        depth = slots.shape[0]

        def copy(i, length):
            slot = lax.rem(i, depth)
            source = streamed_ref.at[rows(i, length)]
            return pltpu.make_async_copy(source, slots.at[slot, pl.ds(0, length)], sems.at[slot])

        for i in range(depth - 1):
            copy(i, width).start()
    high, both = both_halves(x_ref)

    def put(place, i, length, w):
        total = multiplied(high, both, w, 1)
        if kept_place is not None and streamed_place is not None:
            core = lax.rem(lax.axis_index("delay"), 2)
            start = pl.multiple_of(part * (core if place == 0 else 1 - core), part)
        else:
            start = 0
        out_ref[:, pl.ds(start, part), rows(i, length)] = total.reshape(peers, part, length)

    if kept_place is not None:

        def kept_body(i, _):
            put(kept_place, i, width, kept_ref[rows(i, width), :])
            return 0

        lax.fori_loop(0, count, kept_body, 0)
        put(kept_place, count, tail, kept_ref[pl.ds(count * width, tail), :])
    if streamed_place is not None:

        def streamed_body(i, _):
            @pl.when(i + depth - 1 < count)
            def _():
                copy(i + depth - 1, width).start()

            @pl.when(i + depth - 1 == count)
            def _():
                copy(i + depth - 1, tail).start()

            copy(i, width).wait()
            put(streamed_place, i, width, slots[lax.rem(i, depth)])
            return 0

        lax.fori_loop(0, count, streamed_body, 0)
        copy(count, tail).wait()
        put(streamed_place, count, tail, slots[count % depth, pl.ds(0, tail), :])


LIMIT = pltpu.CompilerParams(vmem_limit_bytes=20 * 2**20)
LONG = pl.CostEstimate(flops=2 * 10**10, bytes_accessed=2**20, transcendentals=0)


def tiles(depth, shape):
    return [pltpu.VMEM((depth, *shape), jnp.float32), pltpu.SemaphoreType.DMA((depth,))]


def admit_product(x, operator, kept):
    testing, basis = operator.shape
    columns = x.shape[0] * x.shape[1]
    peers = lax.axis_size("col")
    width = 256
    return pl.pallas_call(
        functools.partial(admit_kernel, width),
        out_shape=jax.ShapeDtypeStruct((peers, columns // peers, basis), jnp.float32),
        in_specs=[IN_VMEM, IN_VMEM if kept else ANYWHERE],
        out_specs=IN_VMEM,
        scratch_shapes=[] if kept else tiles(4, (testing, width)),
        compiler_params=LIMIT,
        name="admit",
    )(x, operator)


def radiate_product(x, kept=None, streamed=None):
    given = [pair for pair in (kept, streamed) if pair is not None]
    testing, basis = given[0][0].shape
    columns = x.shape[0] * x.shape[1]
    peers = lax.axis_size("row")
    width = 256
    places = tuple(None if pair is None else pair[1] for pair in (kept, streamed))
    return pl.pallas_call(
        functools.partial(radiate_kernel, width, places),
        out_shape=jax.ShapeDtypeStruct((peers, len(given) * columns // peers, testing), jnp.float32),
        in_specs=[IN_VMEM] + [IN_VMEM] * (kept is not None) + [ANYWHERE] * (streamed is not None),
        out_specs=IN_VMEM,
        scratch_shapes=[] if streamed is None else tiles(3, (width, basis)),
        compiler_params=LIMIT,
        name="radiate",
    )(x, *[operator for operator, _ in given])


def spread_kernel(x_ref, out_ref):
    for i in range(out_ref.shape[0]):
        out_ref[i] = x_ref[...]


def spread(x, axis):
    return pl.pallas_call(
        spread_kernel,
        out_shape=jax.ShapeDtypeStruct((lax.axis_size(axis), *x.shape), x.dtype),
        in_specs=[IN_VMEM],
        out_specs=IN_VMEM,
        compiler_params=LIMIT,
        cost_estimate=LONG,
        name="spread",
    )(x)


def deduct_kernel(products_ref, given_ref, out_ref):
    row = lax.axis_index("row")
    for i in range(out_ref.shape[0]):
        out_ref[i] = jnp.where(row == i, given_ref[...], 0.0) - products_ref[i]


def deduct(products, given):
    return pl.pallas_call(
        deduct_kernel,
        out_shape=jax.ShapeDtypeStruct(products.shape, products.dtype),
        in_specs=[IN_VMEM, IN_VMEM],
        out_specs=IN_VMEM,
        compiler_params=LIMIT,
        cost_estimate=LONG,
        name="deduct",
    )(products, given)


def prepare_kernel(moments, wide, fresh_ref, *refs):
    *due_refs, slots, sems = refs
    row = lax.axis_index("row")
    core = lax.rem(lax.axis_index("delay"), 2)
    lanes = slots.shape[2]
    per = lanes // wide
    groups = wide // (2 * HALF)
    block = pl.ds(pl.multiple_of(row // per * lanes, lanes), lanes)
    copies = [
        pltpu.make_async_copy(fresh_ref.at[moment, :, block], slots.at[n], sems.at[n])
        for n, moment in enumerate(moments)
    ]
    for copy in copies:
        copy.start()

    def rows_of(ref, which, base):
        pieces = []
        for g in range(groups):
            start = pl.multiple_of(base + (2 * g + which) * HALF, HALF)
            pieces.append(ref[pl.ds(start, HALF), :])
        return jnp.concatenate(pieces, axis=0)

    if len(due_refs) > 2:
        due_ref, fresh_out, mine_out, leaving_out, turned = due_refs
        mine_out[...] = rows_of(due_ref, core, 0)
        leaving_out[...] = rows_of(due_ref, 1 - core, 0)
    else:
        fresh_out, turned = due_refs
    for n, copy in enumerate(copies):
        copy.wait()
        turned[...] = slots[n].T
        fresh_out[n] = rows_of(turned, core, lax.rem(row, per) * wide)


def prepared(excitation, moments, wide, due=None):
    testing = excitation.shape[1]
    half = jax.ShapeDtypeStruct((wide // 2, testing), jnp.float32)
    fresh = jax.ShapeDtypeStruct((len(moments), wide // 2, testing), jnp.float32)
    out = (fresh,) if due is None else (fresh, half, half)
    given = () if due is None else (due,)
    return pl.pallas_call(
        functools.partial(prepare_kernel, moments, wide),
        out_shape=out,
        in_specs=[ANYWHERE] + [IN_VMEM] * len(given),
        out_specs=(IN_VMEM,) * len(out),
        scratch_shapes=[
            pltpu.VMEM((128, testing), jnp.float32),
            pltpu.VMEM((len(moments), testing, 128), jnp.float32),
            pltpu.SemaphoreType.DMA((len(moments),)),
        ],
        compiler_params=pltpu.CompilerParams(vmem_limit_bytes=60 * 2**20),
        name="prepare",
    )(excitation, *given)


def settle_kernel(parts_ref, gain_ref, out_ref):
    sheet = parts_ref[0]
    for i in range(1, parts_ref.shape[0]):
        sheet = sheet + parts_ref[i]
    out_ref[...] = sheet / (1.0 + gain_ref[...] * sheet * sheet)


def settled(parts, gain):
    return pl.pallas_call(
        settle_kernel,
        out_shape=jax.ShapeDtypeStruct(parts.shape[1:], parts.dtype),
        in_specs=[IN_VMEM, IN_VMEM],
        out_specs=IN_VMEM,
        compiler_params=LIMIT,
        name="settle",
    )(parts, gain)


def exchanged(x, axis):
    return lax.all_to_all(x, axis, 0, 0, tiled=True)


def gathered(x, axis):
    return exchanged(spread(x, axis), axis)


def admitted(driving, operator, gain, kept):
    return settled(exchanged(admit_product(driving, operator, kept), "col"), gain)


def radiated(current_part, **operators):
    return exchanged(radiate_product(gathered(current_part, "col"), **operators), "row").sum(axis=0)


def driven(products, given):
    size = lax.axis_size("row")
    total = deduct(products, given)
    near = [(i, i ^ 1) for i in range(size)]
    wrap = [(i, (i + 1 if i % 2 else i - 1) % size) for i in range(size)]
    first, second = total[: size // 2], total[size // 2 :]
    for one, two in ((near, wrap), (wrap, near)):
        came = lax.ppermute(first, "row", one), lax.ppermute(second, "row", two)
        first, second = first + came[0], second + came[1]
    return jnp.concatenate([first, second], axis=0)


def local(operators, excitation, pending, sheet_gain):
    own = operators[0]
    basis = own.shape[1]
    delay = lax.axis_index("delay")
    core = delay % 2
    gain = sheet_gain[None, :]
    wide = pending.shape[2]
    groups = wide // (2 * HALF)

    def join(first, second):
        parts = [x.reshape(groups, 1, HALF, x.shape[-1]) for x in (first, second)]
        return jnp.concatenate(parts, axis=1).reshape(wide, first.shape[-1])

    fresh, mine, leaving = prepared(excitation, (0,), wide, pending[0].T)
    theirs = lax.ppermute(leaving, "delay", SWAP)
    own, leaving = lax.optimization_barrier((own, leaving))
    other = lax.ppermute(own, "delay", SWAP)

    def keep(value, *_):
        return value

    def first_admitted(kept, v, x, y, w):
        return admitted(gathered(x - y, "row"), w, gain, kept)

    blank = jnp.zeros((HALF, basis), jnp.float32)
    cur = lax.cond(delay == 0, functools.partial(first_admitted, True), keep, blank, fresh[0], mine, own)
    excitation, cur = lax.optimization_barrier((excitation, cur))
    (later,) = prepared(excitation, (1, 2), wide)
    cur, theirs, later = lax.optimization_barrier((cur, theirs, later))
    driving = lax.cond(
        delay == 1, lambda v, x, y: gathered(x - y, "row"), keep,
        jnp.zeros((4, 32, 1152), jnp.float32), fresh[0], theirs,
    )
    driving, cur, other = lax.optimization_barrier((driving, cur, other))
    even = jnp.where(core == 0, mine, theirs)
    odd = jnp.where(core == 0, theirs, mine)
    cur = lax.cond(delay == 1, lambda v, x, w: admitted(x, w, gain, False), keep, cur, driving, other)
    which = jnp.minimum(delay, 2)
    currents, arrived = [], []
    near, far, late = [], [], []
    field = jnp.zeros((lax.axis_size("row"), wide // 2, pending.shape[1]), jnp.float32)
    for moment in range(STEPS):
        if moment > 0:
            given = later[moment - 1] - (odd if moment == 1 else late[0])
            cur = lax.switch(
                which,
                [
                    lambda v, x, g, a, b: admitted(driven(x, g), a, gain, True),
                    lambda v, x, g, a, b: admitted(driven(x, g), b, gain, False),
                    keep,
                ],
                blank, field, given, own, other,
            )
        currents.append(cur)
        sent = lax.ppermute(cur, "delay", UP)
        if moment == 1:
            late[0], cur = lax.optimization_barrier((late[0], cur))
        if moment == STEPS - 1:
            part = lax.switch(
                which,
                [
                    lambda v, x, a, b: radiated(x, streamed=(b, 0)),
                    lambda v, x, a, b: radiated(x, kept=(a, 0)),
                    keep,
                ],
                even, cur, own, other,
            )
            sent, done = lax.optimization_barrier((sent, part))
            start = jnp.concatenate([done, done], axis=0)
        else:
            field = lax.switch(
                which,
                [
                    lambda v, x, a, b: radiate_product(gathered(x, "col"), streamed=(b, 0)),
                    lambda v, x, a, b: radiate_product(gathered(x, "col"), kept=(a, 0)),
                    keep,
                ],
                field, cur, own, other,
            )
            sent, field = lax.optimization_barrier((sent, field))
            start = jnp.concatenate([even, odd], axis=0)
        arrived.append(sent)
        pair = lax.cond(
            delay >= 2,
            lambda v, x, a, b: radiated(x, kept=(a, 0), streamed=(b, 1)),
            keep,
            start, sent, own, other,
        )
        near.append(pair[: wide // 2])
        far.append(pair[wide // 2 :])
        if moment == 0:
            late.append(lax.ppermute(even + near[0], "delay", DOWN))
        elif moment == 1:
            late.append(lax.ppermute(odd + near[1] + far[0], "delay", DOWN))

    held = jnp.where(delay < 2, jnp.stack(currents), jnp.stack(arrived))
    swapped = lax.ppermute(held, "delay", SWAP)
    first = jnp.where(core == 0, held, swapped)
    second = jnp.where(core == 0, swapped, held)
    outputs = jnp.swapaxes(jnp.concatenate([first, second], axis=1), 1, 2)

    slot_zero = late[1] + part
    slot_one = near[2] + far[1]
    slot_two = far[2]
    leaving = jnp.where(delay == 1, slot_zero, jnp.where(delay == 2, slot_one, slot_two))
    came = lax.ppermute(leaving, "delay", ((1, 0), (2, 1), (3, 2)))
    crossed = lax.ppermute(slot_one, "delay", ((3, 1),))
    low = jnp.where(delay == 0, slot_zero, jnp.where(delay == 1, came, slot_two))
    high = jnp.where(delay == 1, crossed, came)
    remaining = jnp.where(delay < 3, join(low, high), 0.0)
    return outputs, remaining.T[None]


def solution(mesh):
    in_specs = (P("delay", "col", "row"), P(None, "col", None), P("delay", "col", "row"), P("row"))
    out_specs = (P(None, "row", "col"), P("delay", "col", "row"))
    return jax.shard_map(local, mesh=mesh, in_specs=in_specs, out_specs=out_specs, check_vma=False)
```

```python
import functools

import jax
import jax.numpy as jnp
from jax import lax
from jax.experimental import pallas as pl
from jax.experimental.pallas import tpu as pltpu
from jax.sharding import PartitionSpec as P

STEPS = 3
HALF = 16
SWAP = ((0, 1), (1, 0), (2, 3), (3, 2))
UP = ((0, 2), (1, 3))
DOWN = ((2, 0), (3, 1))


IN_VMEM = pl.BlockSpec(memory_space=pltpu.VMEM)
ANYWHERE = pl.BlockSpec(memory_space=pl.ANY)


def halves(x):
    high = x.astype(jnp.bfloat16)
    return high, (x - high.astype(jnp.float32)).astype(jnp.bfloat16)


def fetched(count, slots, sems, source):
    depth = slots.shape[0]

    def copy(i):
        slot = lax.rem(i, depth)
        return pltpu.make_async_copy(source(i), slots.at[slot], sems.at[slot])

    def start():
        for i in range(depth - 1):
            copy(i).start()

    def take(i):
        @pl.when(i + depth - 1 < count)
        def _():
            copy(i + depth - 1).start()

        copy(i).wait()
        return slots[lax.rem(i, depth)]

    return start, take


def both_halves(x_ref):
    groups, columns, length = x_ref.shape
    high, low = halves(x_ref[...].reshape(groups * columns, length))
    return high, jnp.concatenate([high, low], axis=0)


def multiplied(high, both, w, over):
    w_high, w_low = halves(w)
    over = (((1,), (over,)), ((), ()))
    main = lax.dot_general(both, w_high, over, preferred_element_type=jnp.float32)
    rest = lax.dot_general(high, w_low, over, preferred_element_type=jnp.float32)
    whole = high.shape[0]
    return main[:whole] + main[whole:] + rest


def admit_kernel(width, x_ref, w_ref, out_ref, *scratch):
    peers, part, basis = out_ref.shape
    count = basis // width

    def lanes(i):
        return pl.ds(pl.multiple_of(i * width, width), width)

    if scratch:
        start, take = fetched(count, *scratch, lambda i: w_ref.at[:, lanes(i)])
        start()
    else:
        take = lambda i: w_ref[:, lanes(i)]
    high, both = both_halves(x_ref)

    def body(i, _):
        out_ref[:, :, lanes(i)] = multiplied(high, both, take(i), 0).reshape(peers, part, width)
        return 0

    lax.fori_loop(0, count, body, 0)


def radiate_kernel(width, places, x_ref, *refs):
    kept_place, streamed_place = places
    refs = list(refs)
    kept_ref = refs.pop(0) if kept_place is not None else None
    streamed_ref = refs.pop(0) if streamed_place is not None else None
    out_ref, *scratch = refs
    peers, _, testing = out_ref.shape
    part = x_ref.shape[0] * x_ref.shape[1] // peers
    count, tail = divmod(testing, width)

    def rows(i, length):
        return pl.ds(pl.multiple_of(i * width, width), length)

    if scratch:
        slots, sems = scratch
        depth = slots.shape[0]

        def copy(i, length):
            slot = lax.rem(i, depth)
            source = streamed_ref.at[rows(i, length)]
            return pltpu.make_async_copy(source, slots.at[slot, pl.ds(0, length)], sems.at[slot])

        for i in range(depth - 1):
            copy(i, width).start()
    high, both = both_halves(x_ref)

    def put(place, i, length, w):
        total = multiplied(high, both, w, 1)
        if kept_place is not None and streamed_place is not None:
            core = lax.rem(lax.axis_index("delay"), 2)
            start = pl.multiple_of(part * (core if place == 0 else 1 - core), part)
        else:
            start = 0
        out_ref[:, pl.ds(start, part), rows(i, length)] = total.reshape(peers, part, length)

    if kept_place is not None:

        def kept_body(i, _):
            put(kept_place, i, width, kept_ref[rows(i, width), :])
            return 0

        lax.fori_loop(0, count, kept_body, 0)
        put(kept_place, count, tail, kept_ref[pl.ds(count * width, tail), :])
    if streamed_place is not None:

        def streamed_body(i, _):
            @pl.when(i + depth - 1 < count)
            def _():
                copy(i + depth - 1, width).start()

            @pl.when(i + depth - 1 == count)
            def _():
                copy(i + depth - 1, tail).start()

            copy(i, width).wait()
            put(streamed_place, i, width, slots[lax.rem(i, depth)])
            return 0

        lax.fori_loop(0, count, streamed_body, 0)
        copy(count, tail).wait()
        put(streamed_place, count, tail, slots[count % depth, pl.ds(0, tail), :])


LIMIT = pltpu.CompilerParams(vmem_limit_bytes=20 * 2**20)
LONG = pl.CostEstimate(flops=2 * 10**10, bytes_accessed=2**20, transcendentals=0)


def tiles(depth, shape):
    return [pltpu.VMEM((depth, *shape), jnp.float32), pltpu.SemaphoreType.DMA((depth,))]


def admit_product(x, operator, kept):
    testing, basis = operator.shape
    columns = x.shape[0] * x.shape[1]
    peers = lax.axis_size("col")
    width = 256
    return pl.pallas_call(
        functools.partial(admit_kernel, width),
        out_shape=jax.ShapeDtypeStruct((peers, columns // peers, basis), jnp.float32),
        in_specs=[IN_VMEM, IN_VMEM if kept else ANYWHERE],
        out_specs=IN_VMEM,
        scratch_shapes=[] if kept else tiles(4, (testing, width)),
        compiler_params=LIMIT,
        name="admit",
    )(x, operator)


def radiate_product(x, kept=None, streamed=None):
    given = [pair for pair in (kept, streamed) if pair is not None]
    testing, basis = given[0][0].shape
    columns = x.shape[0] * x.shape[1]
    peers = lax.axis_size("row")
    width = 256
    places = tuple(None if pair is None else pair[1] for pair in (kept, streamed))
    return pl.pallas_call(
        functools.partial(radiate_kernel, width, places),
        out_shape=jax.ShapeDtypeStruct((peers, len(given) * columns // peers, testing), jnp.float32),
        in_specs=[IN_VMEM] + [IN_VMEM] * (kept is not None) + [ANYWHERE] * (streamed is not None),
        out_specs=IN_VMEM,
        scratch_shapes=[] if streamed is None else tiles(3, (width, basis)),
        compiler_params=LIMIT,
        name="radiate",
    )(x, *[operator for operator, _ in given])


def spread_kernel(x_ref, out_ref):
    for i in range(out_ref.shape[0]):
        out_ref[i] = x_ref[...]


def spread(x, axis):
    return pl.pallas_call(
        spread_kernel,
        out_shape=jax.ShapeDtypeStruct((lax.axis_size(axis), *x.shape), x.dtype),
        in_specs=[IN_VMEM],
        out_specs=IN_VMEM,
        compiler_params=LIMIT,
        cost_estimate=LONG,
        name="spread",
    )(x)


def deduct_kernel(products_ref, given_ref, out_ref):
    row = lax.axis_index("row")
    for i in range(out_ref.shape[0]):
        out_ref[i] = jnp.where(row == i, given_ref[...], 0.0) - products_ref[i]


def deduct(products, given):
    return pl.pallas_call(
        deduct_kernel,
        out_shape=jax.ShapeDtypeStruct(products.shape, products.dtype),
        in_specs=[IN_VMEM, IN_VMEM],
        out_specs=IN_VMEM,
        compiler_params=LIMIT,
        cost_estimate=LONG,
        name="deduct",
    )(products, given)


def prepare_kernel(moments, wide, fresh_ref, *refs):
    *due_refs, slots, sems = refs
    row = lax.axis_index("row")
    core = lax.rem(lax.axis_index("delay"), 2)
    lanes = slots.shape[2]
    per = lanes // wide
    groups = wide // (2 * HALF)
    block = pl.ds(pl.multiple_of(row // per * lanes, lanes), lanes)
    copies = [
        pltpu.make_async_copy(fresh_ref.at[moment, :, block], slots.at[n], sems.at[n])
        for n, moment in enumerate(moments)
    ]
    for copy in copies:
        copy.start()

    def rows_of(ref, which, base):
        pieces = []
        for g in range(groups):
            start = pl.multiple_of(base + (2 * g + which) * HALF, HALF)
            pieces.append(ref[pl.ds(start, HALF), :])
        return jnp.concatenate(pieces, axis=0)

    if len(due_refs) > 2:
        due_ref, fresh_out, mine_out, leaving_out, turned = due_refs
        mine_out[...] = rows_of(due_ref, core, 0)
        leaving_out[...] = rows_of(due_ref, 1 - core, 0)
    else:
        fresh_out, turned = due_refs
    for n, copy in enumerate(copies):
        copy.wait()
        turned[...] = slots[n].T
        fresh_out[n] = rows_of(turned, core, lax.rem(row, per) * wide)


def prepared(excitation, moments, wide, due=None):
    testing = excitation.shape[1]
    half = jax.ShapeDtypeStruct((wide // 2, testing), jnp.float32)
    fresh = jax.ShapeDtypeStruct((len(moments), wide // 2, testing), jnp.float32)
    out = (fresh,) if due is None else (fresh, half, half)
    given = () if due is None else (due,)
    return pl.pallas_call(
        functools.partial(prepare_kernel, moments, wide),
        out_shape=out,
        in_specs=[ANYWHERE] + [IN_VMEM] * len(given),
        out_specs=(IN_VMEM,) * len(out),
        scratch_shapes=[
            pltpu.VMEM((128, testing), jnp.float32),
            pltpu.VMEM((len(moments), testing, 128), jnp.float32),
            pltpu.SemaphoreType.DMA((len(moments),)),
        ],
        compiler_params=pltpu.CompilerParams(vmem_limit_bytes=60 * 2**20),
        name="prepare",
    )(excitation, *given)


def settle_kernel(parts_ref, gain_ref, out_ref):
    sheet = parts_ref[0]
    for i in range(1, parts_ref.shape[0]):
        sheet = sheet + parts_ref[i]
    out_ref[...] = sheet / (1.0 + gain_ref[...] * sheet * sheet)


def settled(parts, gain):
    return pl.pallas_call(
        settle_kernel,
        out_shape=jax.ShapeDtypeStruct(parts.shape[1:], parts.dtype),
        in_specs=[IN_VMEM, IN_VMEM],
        out_specs=IN_VMEM,
        compiler_params=LIMIT,
        name="settle",
    )(parts, gain)


def exchanged(x, axis):
    return lax.all_to_all(x, axis, 0, 0, tiled=True)


def gathered(x, axis):
    return exchanged(spread(x, axis), axis)


def admitted(driving, operator, gain, kept):
    return settled(exchanged(admit_product(driving, operator, kept), "col"), gain)


def radiated(current_part, **operators):
    return exchanged(radiate_product(gathered(current_part, "col"), **operators), "row").sum(axis=0)


def driven(products, given, flip=False):
    size = lax.axis_size("row")
    total = deduct(products, given)
    near = [(i, i ^ 1) for i in range(size)]
    wrap = [(i, (i + 1 if i % 2 else i - 1) % size) for i in range(size)]
    if flip:
        near, wrap = wrap, near
    first, second = total[: size // 2], total[size // 2 :]
    for one, two in ((near, wrap), (wrap, near)):
        came = lax.ppermute(first, "row", one), lax.ppermute(second, "row", two)
        first, second = first + came[0], second + came[1]
    return jnp.concatenate([first, second], axis=0)


def local(operators, excitation, pending, sheet_gain):
    own = operators[0]
    basis = own.shape[1]
    delay = lax.axis_index("delay")
    core = delay % 2
    gain = sheet_gain[None, :]
    wide = pending.shape[2]
    groups = wide // (2 * HALF)

    def join(first, second):
        parts = [x.reshape(groups, 1, HALF, x.shape[-1]) for x in (first, second)]
        return jnp.concatenate(parts, axis=1).reshape(wide, first.shape[-1])

    fresh, mine, leaving = prepared(excitation, (0,), wide, pending[0].T)
    theirs = lax.ppermute(leaving, "delay", SWAP)
    own, leaving = lax.optimization_barrier((own, leaving))
    other = lax.ppermute(own, "delay", SWAP)

    def keep(value, *_):
        return value

    def first_admitted(kept, v, x, y, w):
        return admitted(gathered(x - y, "row"), w, gain, kept)

    blank = jnp.zeros((HALF, basis), jnp.float32)
    cur = lax.cond(delay == 0, functools.partial(first_admitted, True), keep, blank, fresh[0], mine, own)
    excitation, cur = lax.optimization_barrier((excitation, cur))
    (later,) = prepared(excitation, (1, 2), wide)
    cur, theirs, later = lax.optimization_barrier((cur, theirs, later))
    driving = lax.cond(
        delay == 1, lambda v, x, y: gathered(x - y, "row"), keep,
        jnp.zeros((4, 32, 1152), jnp.float32), fresh[0], theirs,
    )
    driving, cur, other = lax.optimization_barrier((driving, cur, other))
    even = jnp.where(core == 0, mine, theirs)
    odd = jnp.where(core == 0, theirs, mine)
    cur = lax.cond(delay == 1, lambda v, x, w: admitted(x, w, gain, False), keep, cur, driving, other)
    which = jnp.minimum(delay, 2)
    currents, arrived = [], []
    near, far, late = [], [], []
    field = jnp.zeros((lax.axis_size("row"), wide // 2, pending.shape[1]), jnp.float32)
    for moment in range(STEPS):
        if moment > 0:
            given = later[moment - 1] - (odd if moment == 1 else late[0])
            cur = lax.switch(
                which,
                [
                    lambda v, x, g, a, b: admitted(driven(x, g), a, gain, True),
                    lambda v, x, g, a, b: admitted(driven(x, g, True), b, gain, False),
                    keep,
                ],
                blank, field, given, own, other,
            )
        currents.append(cur)
        sent = lax.ppermute(cur, "delay", UP)
        if moment == 1:
            late[0], cur = lax.optimization_barrier((late[0], cur))
        if moment == STEPS - 1:
            part = lax.switch(
                which,
                [
                    lambda v, x, a, b: radiated(x, streamed=(b, 0)),
                    lambda v, x, a, b: radiated(x, kept=(a, 0)),
                    keep,
                ],
                even, cur, own, other,
            )
            sent, done = lax.optimization_barrier((sent, part))
            start = jnp.concatenate([done, done], axis=0)
        else:
            field = lax.switch(
                which,
                [
                    lambda v, x, a, b: radiate_product(gathered(x, "col"), streamed=(b, 0)),
                    lambda v, x, a, b: radiate_product(gathered(x, "col"), kept=(a, 0)),
                    keep,
                ],
                field, cur, own, other,
            )
            sent, field = lax.optimization_barrier((sent, field))
            start = jnp.concatenate([even, odd], axis=0)
        arrived.append(sent)
        pair = lax.cond(
            delay >= 2,
            lambda v, x, a, b: radiated(x, kept=(a, 0), streamed=(b, 1)),
            keep,
            start, sent, own, other,
        )
        near.append(pair[: wide // 2])
        far.append(pair[wide // 2 :])
        if moment == 0:
            late.append(lax.ppermute(even + near[0], "delay", DOWN))
        elif moment == 1:
            late.append(lax.ppermute(odd + near[1] + far[0], "delay", DOWN))

    held = jnp.where(delay < 2, jnp.stack(currents), jnp.stack(arrived))
    swapped = lax.ppermute(held, "delay", SWAP)
    first = jnp.where(core == 0, held, swapped)
    second = jnp.where(core == 0, swapped, held)
    outputs = jnp.swapaxes(jnp.concatenate([first, second], axis=1), 1, 2)

    slot_zero = late[1] + part
    slot_one = near[2] + far[1]
    slot_two = far[2]
    leaving = jnp.where(delay == 1, slot_zero, jnp.where(delay == 2, slot_one, slot_two))
    crossed = lax.ppermute(slot_one, "delay", ((3, 1),))
    came = lax.ppermute(leaving, "delay", ((1, 0), (2, 1), (3, 2)))
    low = jnp.where(delay == 0, slot_zero, jnp.where(delay == 1, came, slot_two))
    high = jnp.where(delay == 1, crossed, came)
    remaining = jnp.where(delay < 3, join(low, high), 0.0)
    return outputs, remaining.T[None]


def solution(mesh):
    in_specs = (P("delay", "col", "row"), P(None, "col", None), P("delay", "col", "row"), P("row"))
    out_specs = (P(None, "row", "col"), P("delay", "col", "row"))
    return jax.shard_map(local, mesh=mesh, in_specs=in_specs, out_specs=out_specs, check_vma=False)
```
